256 devices in a mesh: blk: 64 (over x, z, y_hi), mp: 4 (over y_lo, core).
Axes of the slice: x: 4, y: 4 (y_hi: 2, y_lo: 2; y = y_hi * 2 + y_lo), z: 8, core: 2. Of those that a mesh axis runs over, the one named last changes fastest.
Arguments:
- hidden_in: bfloat16 [8192, 2048], P('blk'), may hold values from -6 to 6
- norm_gain: float32 [2048], replicated, may hold values from 0.25 to 1.75
- norm_bias: float32 [2048], replicated, may hold values from -3 to 3
- w_query: bfloat16 [2048, 2048], P(None, 'mp'), may hold values from -2 to 2
- w_key: bfloat16 [2048, 2048], P(None, 'mp'), may hold values from -0.125 to 0.125
- w_value: bfloat16 [2048, 2048], P(None, 'mp'), may hold values from -0.125 to 0.125
- w_out: bfloat16 [2048, 2048], P('mp'), may hold values from -0.125 to 0.125
- prefix_keys: bfloat16 [64, 128, 2048], P('blk', None, 'mp'), may hold values from -6 to 6
- prefix_values: bfloat16 [64, 128, 2048], P('blk', None, 'mp'), may hold values from -6 to 6
- segment: int32 [64, 128], P('blk'), may hold values from 0 to 3, never falling along the last dimension, each value on 1 to 64 neighbouring positions
- request_group: int32 [64, 4], P('blk'), may hold values from 0 to 3
- block_slot: int32 [64], P('blk'), may hold values from 0 to 63, each once
- block_live: int32 [64], P('blk'), may hold values 0 or 1
Outputs:
- hidden_out: bfloat16 [8192, 2048], P('blk')
The draws below stay inside these ranges and needn't reach their ends.
Inputs may be any that keep to these rules, and one draw needn't show every extreme that they name: Each row of segment counts requests 0 to 3 without falling; each request has 1 to 64 tokens. `block_slot`: each slot once.
All inputs are finite; a program needn't handle non-finite values. No bound on the sum of `block_live` on one device may be relied on, other than what follows from the above.
Results may differ from the reference program's by a relative error of at most 0.009.
Values may be sent and summed in bfloat16 or wider, within the bound.
A program may use at most 128 MiB of HBM per device.

```python
import math
import jax
import jax.numpy as jnp
import numpy as np
from jax import lax

D = 2048
HEADS = 16
HD = 128
SUF_DEV = 128
REQ_DEV = 4
GROUPS = 4
BLOCK_TOK = 128
TOKENS = 8192
BLOCKS = 64


def draw_w_query(key, part):
    scale = 1.0 / jnp.sqrt(jnp.float32(D))
    base = jnp.clip(jax.random.normal(jax.random.fold_in(key, 11), (D, D), jnp.float32), -6.0, 6.0) * scale
    return base.astype(jnp.bfloat16)


def draw_prefix_keys(key, part):
    base = jnp.clip(jax.random.normal(jax.random.fold_in(key, 21), (BLOCKS, BLOCK_TOK, D), jnp.float32), -6.0, 6.0)
    return base.astype(jnp.bfloat16)


def with_ends(drawn, stream_key, least, top_value):
    longest = drawn.shape.index(max(drawn.shape))
    spots = []
    for shift in (0, 1):
        where = [jax.random.randint(jax.random.fold_in(stream_key, axis), (), 0, length) for axis, length in enumerate(drawn.shape)]
        where[longest] = (where[longest] + shift) % drawn.shape[longest]
        spots.append(tuple(where))
    return drawn.at[spots[0]].set(least).at[spots[1]].set(top_value)


def block_levels(stream_key, shape, cuts, smallest, top_value):
    level = 1.0
    for dim, blocks in cuts:
        draws = jax.random.uniform(jax.random.fold_in(jax.random.fold_in(stream_key, 6), dim), (blocks,), jnp.float32, smallest / len(cuts), top_value / len(cuts))
        level = level * jnp.repeat(jnp.exp(draws), shape[dim] // blocks).reshape((-1,) + (1,) * (len(shape) - 1 - dim))
    return level


def split_up(amount, total, reach, skew):
    loads = [(1 << 20) // math.isqrt(grade ** skew) + 1 for grade in range(2, amount + 1)]
    surplus, given = total - reach - (amount - 1), [1] * (amount - 1)
    while surplus > 0:
        free = [i for i in range(amount - 1) if given[i] < reach]
        whole, left = sum([loads[i] for i in free]), surplus
        for i in free:
            addition = min(reach - given[i], max(1, left * loads[i] // whole), surplus)
            given[i] = given[i] + addition
            surplus = surplus - addition
    return np.array([reach] + given)


def ragged(key, count, total, limit, slope):
    if count == 2:
        one = jax.random.randint(key, (), max(1, total - limit), min(limit, total - 1) + 1)
        return jnp.stack([one, total - one])
    tallies = jnp.asarray(split_up(count, total, limit, slope), jnp.int32)
    couples = (count - 1) // 2
    source_of, receiver = tallies[1:1 + 2 * couples:2], tallies[2:2 + 2 * couples:2]
    room = jnp.minimum(source_of - 1, limit - receiver)
    passed = jax.random.randint(jax.random.fold_in(key, 1), (couples,), 0, 1 << 20) % (room + 1)
    tallies = tallies.at[1:1 + 2 * couples:2].set(source_of - passed).at[2:2 + 2 * couples:2].set(receiver + passed)
    return tallies[jax.random.permutation(jax.random.fold_in(key, 2), count)]


def gaussian(own_key, shape, deviation, limit, pieces=(), kind=jnp.bfloat16):
    drawn = deviation * jax.random.normal(own_key, shape, jnp.float32)
    if pieces:
        drawn = drawn * block_levels(own_key, shape, pieces, -0.22, 0.18)
    return jnp.clip(drawn, -limit, limit).astype(kind)


def setup_inputs(seed: int = 0) -> dict:
    seeds = jax.random.split(jax.random.key(seed), 14)
    return {
        "hidden_in": gaussian(seeds[0], (TOKENS, D), 1.0, 6.0, ((0, 64),)),
        "norm_gain": jnp.clip(1.0 + 0.15 * jax.random.normal(seeds[1], (D,), jnp.float32), 0.25, 1.75),
        "norm_bias": gaussian(seeds[2], (D,), 0.5, 3.0, (), jnp.float32),
        "w_query": draw_w_query(jax.random.fold_in(seeds[13], 71), 0),
        "w_key": gaussian(seeds[4], (D, D), D ** -0.5, 0.125, ((1, 4),)),
        "w_value": gaussian(seeds[5], (D, D), D ** -0.5, 0.125, ((1, 4),)),
        "w_out": gaussian(seeds[6], (D, D), D ** -0.5, 0.125, ((0, 4),)),
        "prefix_keys": draw_prefix_keys(jax.random.fold_in(seeds[13], 71), 0),
        "prefix_values": gaussian(seeds[8], (BLOCKS, BLOCK_TOK, D), 1.0, 6.0, ((0, 64), (2, 4))),
        "segment": jax.vmap(lambda own: jnp.searchsorted(jnp.cumsum(ragged(own, REQ_DEV, SUF_DEV, SUF_DEV // 2, 2)), jnp.arange(SUF_DEV), side="right"))(jax.random.split(seeds[9], BLOCKS)).reshape((BLOCKS, SUF_DEV)).astype(jnp.int32),
        "request_group": with_ends(jax.random.randint(seeds[10], (BLOCKS, REQ_DEV), 0, GROUPS), jax.random.fold_in(seeds[10], 1), 0, GROUPS - 1).astype(jnp.int32),
        "block_slot": jax.random.permutation(seeds[11], BLOCKS).astype(jnp.int32),
        "block_live": with_ends((jax.random.randint(seeds[12], (BLOCKS,), 0, 4) < 3).astype(jnp.int32), jax.random.fold_in(seeds[12], 1), 0, 1),
    }


big = 1e+30

def layer_norm(values, gain, bias):
    mean = lax.optimization_barrier(jnp.mean(values, axis=-1, keepdims=True))
    centred = values - mean
    var = lax.optimization_barrier(jnp.mean(centred * centred, axis=-1, keepdims=True))
    return centred * lax.rsqrt(var + 1e-05) * gain + bias

def reference(hidden_in, norm_gain, norm_bias, w_query, w_key, w_value, w_out, prefix_keys, prefix_values, segment, request_group, block_slot, block_live):
    inputs = hidden_in.astype(jnp.float32)
    normed = layer_norm(inputs, norm_gain, norm_bias).astype(jnp.bfloat16)
    query = (jnp.dot(normed, w_query, preferred_element_type=jnp.float32) / jnp.sqrt(jnp.float32(HD))).astype(jnp.bfloat16)
    key = jnp.dot(normed, w_key, preferred_element_type=jnp.float32).astype(jnp.bfloat16)
    value = jnp.dot(normed, w_value, preferred_element_type=jnp.float32).astype(jnp.bfloat16)
    block_group = jnp.where(block_live == 1, block_slot * GROUPS // BLOCKS, -1)
    key_tags = jnp.repeat(block_group, BLOCK_TOK)
    all_keys = prefix_keys.reshape(BLOCKS * BLOCK_TOK, HEADS, HD).astype(jnp.float32)
    all_values = prefix_values.reshape(BLOCKS * BLOCK_TOK, HEADS, HD).astype(jnp.float32)
    places = jnp.arange(SUF_DEV)

    def one_row(row):
        start = (row * SUF_DEV).astype(jnp.int32)
        q_rows = lax.dynamic_slice_in_dim(query, start, SUF_DEV, 0).reshape(SUF_DEV, HEADS, HD).astype(jnp.float32)
        k_rows = lax.dynamic_slice_in_dim(key, start, SUF_DEV, 0).reshape(SUF_DEV, HEADS, HD).astype(jnp.float32)
        v_rows = lax.dynamic_slice_in_dim(value, start, SUF_DEV, 0).reshape(SUF_DEV, HEADS, HD).astype(jnp.float32)
        seg_row = segment[row]
        groups_row = request_group[row]
        token_group = lax.optimization_barrier(jnp.sum(jnp.where(seg_row[:, None] == jnp.arange(REQ_DEV)[None, :], groups_row[None, :], 0), axis=1))
        pre_scores = jnp.einsum('qhd,khd->hqk', q_rows, all_keys)
        pre_mask = token_group[:, None] == key_tags[None, :]
        loc_scores = jnp.einsum('qhd,khd->hqk', q_rows, k_rows)
        loc_mask = (seg_row[:, None] == seg_row[None, :]) & (places[None, :] <= places[:, None])
        scores = jnp.concatenate([pre_scores, loc_scores], axis=2)
        mask = jnp.concatenate([pre_mask, loc_mask], axis=1)[None]
        top = lax.optimization_barrier(jnp.max(jnp.where(mask, scores, -big), axis=2, keepdims=True))
        weights = jnp.where(mask, jnp.exp(scores - top), 0.0)
        total = lax.optimization_barrier(jnp.sum(weights, axis=2))
        rounded = weights.astype(jnp.bfloat16).astype(jnp.float32)
        both_values = jnp.concatenate([all_values, v_rows], axis=0)
        summed = jnp.einsum('hqk,khd->hqd', rounded, both_values)
        attended = (summed / total[..., None]).astype(jnp.bfloat16)
        return jnp.transpose(attended, (1, 0, 2)).reshape(SUF_DEV, D)
    attended = lax.map(one_row, jnp.arange(BLOCKS, dtype=jnp.int32)).reshape(TOKENS, D)
    branch = jnp.dot(attended, w_out, preferred_element_type=jnp.float32)
    return (inputs + branch).astype(jnp.bfloat16)
```

```python
import jax
import jax.numpy as jnp
from jax import lax
from jax.experimental import pallas as pl
from jax.experimental.pallas import tpu as pltpu
from jax.sharding import PartitionSpec as P

MESH = pl.DeviceIdType.MESH
HD = 128
GROUPS = 4
XS, ZS, YS = 4, 8, 2
ROWS = 128
TOK = 128
UNIT = 272
BIG = 1e30
CH = 4

f32 = jnp.float32
bf16 = jnp.bfloat16


def dot_t(a, b):
    return lax.dot_general(a, b, (((1,), (1,)), ((), ())), preferred_element_type=f32)


def kernel(
    hid_hbm, gain_ref, bias_ref, wq_hbm, wk_hbm, wv_hbm, wo_hbm, pk_hbm, pv_hbm,
    seg_ref, rg_ref, slot_ref, live_ref, out_ref,
    hid, wq, wk, wv, wo, nrm, stage, kv, qst, qbuf, gst, gbuf, oh, kc, vc, acc, mx,
    knew, vnew, sacc, smx, stot, rst, rbuf, sst, sbuf, att, part, s1, r1, s2, r2,
    w_sem, st_sem, a_ssem, a_rsem, z_ssem, z_rsem, q_ssem, q_rsem, g_ssem, g_rsem,
    r_ssem, r_rsem, t_ssem, t_rsem, m_ssem, m_rsem,
):
    blk = lax.axis_index("blk")
    mp = lax.axis_index("mp")
    y = blk % YS
    z = (blk // YS) % ZS
    x = blk // (YS * ZS)
    core = mp % 2
    ylo = mp // 2

    def at(px, pz, py):
        return {"blk": (px * ZS + pz) * YS + py}

    def plus(ox, oy):
        return at((x + ox) % XS, z, (y + oy) % YS)

    def minus(ox, oy):
        return at((x + XS - ox) % XS, z, (y + oy) % YS)

    right, left = at(x, (z + 1) % ZS, y), at(x, (z + ZS - 1) % ZS, y)
    mate = {"mp": mp + 1 - 2 * core}
    across = {"mp": mp + 2 - 4 * ylo}
    peers = [(ox, oy) for oy in range(YS) for ox in range(XS) if (ox, oy) != (0, 0)]

    def rdma(src, dst, ssem, rsem, dev):
        return pltpu.make_async_remote_copy(
            src_ref=src, dst_ref=dst, send_sem=ssem, recv_sem=rsem,
            device_id=dev, device_id_type=MESH,
        )

    pending = []

    def send(*args):
        copy = rdma(*args)
        copy.start()
        pending.append(copy)
        return copy

    staged = []
    for o in range(XS):
        col = pl.ds(pl.multiple_of(((x + o) % XS) * HD, HD), HD)
        base = kv.at[0, 0] if o == 0 else stage.at[o - 1]
        for i, src in enumerate((pk_hbm, pv_hbm)):
            rows = pl.ds(0, TOK) if i == 0 else pl.ds(TOK + 16, TOK)
            c = pltpu.make_async_copy(src.at[0, :, col], base.at[rows, :], st_sem.at[o, i])
            c.start()
            staged.append(c)
    loads = []
    for i, (src, dst) in enumerate(
        ((hid_hbm, hid), (wq_hbm, wq), (wk_hbm, wk), (wv_hbm, wv), (wo_hbm, wo))
    ):
        c = pltpu.make_async_copy(src, dst, w_sem.at[i])
        c.start()
        loads.append(c)

    barrier = pltpu.get_barrier_semaphore()
    friends = [plus(ox, oy) for ox, oy in peers] + [right, left, mate, across]
    for d in friends:
        pl.semaphore_signal(barrier, inc=1, device_id=d, device_id_type=MESH)

    tag = jnp.where(live_ref[0] == 1, slot_ref[0] * GROUPS // (XS * ZS * YS), -1)
    lane16 = lax.broadcasted_iota(jnp.int32, (16, HD), 1)
    mask_rows = jnp.where(lane16 == tag, 0.0, -BIG).astype(bf16)
    for o in range(XS):
        if o == 0:
            kv[0, 0, TOK:TOK + 16, :] = mask_rows
        else:
            stage[o - 1, TOK:TOK + 16, :] = mask_rows
    seg = seg_ref[...]
    grp = jnp.zeros((1, TOK), f32)
    for r in range(rg_ref.shape[1]):
        grp = jnp.where(seg == r, rg_ref[0, r].astype(f32), grp)
    grp8 = jnp.broadcast_to(grp, (8, TOK))
    gst[...] = grp8
    gbuf[0] = grp8
    vc[:, HD:] = jnp.ones((4 * TOK, HD), bf16)

    pl.semaphore_wait(barrier, len(friends))

    for c in staged:
        c.wait()
    a2a = {}
    for o in (1, 3, 2):
        a2a[o] = send(stage.at[o - 1], kv.at[0, o], a_ssem.at[o], a_rsem.at[o], plus(o, 0))

    ring = {}

    def push(u, b, to, dev):
        ring[to, b] = send(kv.at[u, b], kv.at[to, b], z_ssem.at[to, b], z_rsem.at[to, b], dev)

    push(0, 0, 1, right)
    push(0, 0, 7, left)
    gcopy = []
    for ox, oy in peers:
        s = oy * XS + ox
        gcopy.append(send(gst, gbuf.at[s], g_ssem.at[s], g_rsem.at[s], plus(ox, oy)))

    loads[0].wait()

    def norm(i, _):
        rows = pl.ds(pl.multiple_of(i * 16, 16), 16)
        v = hid[rows, :].astype(f32)
        c = v - jnp.mean(v, axis=1, keepdims=True)
        var = jnp.mean(c * c, axis=1, keepdims=True)
        nrm[rows, :] = (c * lax.rsqrt(var + 1e-05) * gain_ref[...] + bias_ref[...]).astype(bf16)
        return 0

    lax.fori_loop(0, ROWS // 16, norm, 0)

    for b in (1, 3, 2):
        a2a[b].wait_recv()
        push(0, b, 1, right)
        push(0, b, 7, left)

    loads[1].wait()
    q = jnp.dot(nrm[...], wq[...], preferred_element_type=f32) / jnp.sqrt(f32(HD))
    for h in range(4):
        qst[h] = q[:, h * HD:(h + 1) * HD].astype(bf16)
    qbuf[0] = qst[x]
    qcopy = []
    for ox, oy in peers:
        s = oy * XS + ox
        qcopy.append(
            send(qst.at[(x + ox) % XS], qbuf.at[s], q_ssem.at[s], q_rsem.at[s], plus(ox, oy))
        )

    def forward(d, b):
        ring[d, b].wait_recv()
        if d < 3 or b in (0, 1):
            push(d, b, d + 1, right)
        ring[8 - d, b].wait_recv()
        if d < 3 or b in (2, 3):
            push(8 - d, b, 7 - d, left)

    order = (0, 1, 3, 2)

    forward(1, order[0])
    forward(1, order[1])
    loads[2].wait()
    k = jnp.dot(nrm[...], wk[...], preferred_element_type=f32)
    for h in range(4):
        knew[h] = k[:, h * HD:(h + 1) * HD].astype(bf16)
    forward(1, order[2])
    forward(1, order[3])
    loads[3].wait()
    v = jnp.dot(nrm[...], wv[...], preferred_element_type=f32)
    for h in range(4):
        vnew[h] = v[:, h * HD:(h + 1) * HD].astype(bf16)

    segb = jnp.broadcast_to(seg.astype(f32), (TOK, TOK))
    segt = segb.T
    row_i = lax.broadcasted_iota(jnp.int32, (TOK, TOK), 0)
    col_i = lax.broadcasted_iota(jnp.int32, (TOK, TOK), 1)
    own = (segb == segt) & (col_i <= row_i)
    for h in range(4):
        s = jnp.where(own, dot_t(qst[h], knew[h]), -BIG)
        top = jnp.max(s, axis=1, keepdims=True)
        w = jnp.where(own, jnp.exp(s - top), 0.0)
        stot[h] = jnp.broadcast_to(jnp.sum(w, axis=1, keepdims=True), (TOK, HD))
        smx[h] = jnp.broadcast_to(top, (TOK, HD))
        sacc[h] = jnp.dot(w.astype(bf16), vnew[h], preferred_element_type=f32)

    for c in gcopy:
        c.wait_recv()
    for s in range(XS * YS):
        hot = jnp.broadcast_to(gbuf[s][0:1, :], (TOK, TOK)) == row_i.astype(f32)
        oh[s] = jnp.where(hot, 1.0, 0.0).T.astype(bf16)

    acc[...] = jnp.zeros_like(acc)
    mx[...] = jnp.full_like(mx, -3e38)
    for c in qcopy:
        c.wait_recv()

    def attend(blocks):
        for i, (u, b) in enumerate(blocks):
            rows = slice(i * TOK, (i + 1) * TOK)
            kc[rows, 0:HD] = kv[u, b, 0:TOK, :]
            kc[rows, HD:] = jnp.concatenate([kv[u, b, TOK:TOK + 16, :]] * 8, axis=0)
            vc[rows, 0:HD] = kv[u, b, TOK + 16:UNIT, :]

        def body(r, _):
            pair = pl.ds(r * 2, 2)
            qq = jnp.concatenate(
                [qbuf[pair].reshape(2 * TOK, HD), oh[pair].reshape(2 * TOK, HD)], axis=1
            )
            s = dot_t(qq, kc[...])
            old = mx[pair].reshape(2 * TOK, HD)
            new = jnp.maximum(old, jnp.broadcast_to(jnp.max(s, axis=1, keepdims=True), old.shape))
            w = jnp.exp(s - jnp.concatenate([new] * 4, axis=1)).astype(bf16)
            keep = jnp.exp(old - new)
            prev = acc[pair].reshape(2 * TOK, 2 * HD)
            res = prev * jnp.concatenate([keep, keep], axis=1) + jnp.dot(
                w, vc[...], preferred_element_type=f32
            )
            acc[pair] = res.reshape(2, TOK, 2 * HD)
            mx[pair] = new.reshape(2, TOK, HD)
            return 0

        lax.fori_loop(0, XS * YS // 2, body, 0)

    attend([(0, b) for b in order])
    for d in (2, 3):
        for i in (0, 2):
            forward(d, order[i])
            forward(d, order[i + 1])
            attend([(d - 1, order[i]), (9 - d, order[i]), (d - 1, order[i + 1]), (9 - d, order[i + 1])])
    for i in (0, 2):
        attend([(3, order[i]), (5, order[i]), (3, order[i + 1]), (5, order[i + 1])])
    for b in range(4):
        ring[4, b].wait_recv()
    attend([(4, b) for b in range(4)])

    lane = lax.broadcasted_iota(jnp.int32, (TOK, HD), 1)
    back = []
    for ox, oy in peers[::-1] + [(0, 0)]:
        s = oy * XS + ox
        res = acc[s]
        stats = jnp.where(lane == 0, mx[s], res[:, HD:]).T[0:8, :]
        if s == 0:
            rbuf[0] = res[:, :HD].astype(bf16)
            sbuf[0] = stats
        else:
            rst[s] = res[:, :HD].astype(bf16)
            sst[s] = stats
            dev = minus(ox, oy)
            back.append(send(rst.at[s], rbuf.at[s], r_ssem.at[s], r_rsem.at[s], dev))
            back.append(send(sst.at[s], sbuf.at[s], t_ssem.at[s], t_rsem.at[s], dev))
    for c in back:
        c.wait_recv()
    st = sbuf[...].reshape(8 * XS * YS, TOK)
    st = jnp.concatenate([st, st], axis=0).T
    for ox in range(XS):
        h = (x + ox) % XS
        i, j = 8 * ox, 8 * (XS + ox)
        m1, l1 = st[:, i:i + 1], st[:, i + 1:i + 2]
        m2, l2 = st[:, j:j + 1], st[:, j + 1:j + 2]
        m3, l3 = smx[h], stot[h]
        top = jnp.maximum(jnp.maximum(m1, m2), m3)
        e1, e2, e3 = jnp.exp(m1 - top), jnp.exp(m2 - top), jnp.exp(m3 - top)
        num = rbuf[ox].astype(f32) * e1 + rbuf[XS + ox].astype(f32) * e2 + sacc[h] * e3
        att[h] = (num / (l1 * e1 + l2 * e2 + l3 * e3)).astype(bf16)

    loads[4].wait()
    attended = jnp.concatenate([att[h] for h in range(4)], axis=1)
    half = ROWS // 2
    mine = pl.ds(pl.multiple_of(core * half, half), half)
    other = pl.ds(pl.multiple_of((1 - core) * half, half), half)
    wide = out_ref.shape[1] // CH
    cols = [slice(c * wide, (c + 1) * wide) for c in range(CH)]
    first, second, third = [], [], []
    for c in range(CH):
        part[:, cols[c]] = jnp.dot(attended, wo[:, cols[c]], preferred_element_type=f32)
        s1[c] = part[other, cols[c]].astype(bf16)
        first.append(send(s1.at[c], r1.at[c], m_ssem.at[0, c], m_rsem.at[0, c], mate))
    for c in range(CH):
        first[c].wait_recv()
        s2[c] = (part[mine, cols[c]] + r1[c].astype(f32)).astype(bf16)
        second.append(send(s2.at[c], r2.at[c], m_ssem.at[1, c], m_rsem.at[1, c], across))
    for c in range(CH):
        second[c].wait_recv()
        total = s2[c].astype(f32) + r2[c].astype(f32)
        out_ref[mine, cols[c]] = (hid[mine, cols[c]].astype(f32) + total).astype(bf16)
        spot = out_ref.at[mine, pl.ds(c * wide, wide)]
        third.append(send(spot, spot, m_ssem.at[2, c], m_rsem.at[2, c], mate))
    for c in third:
        c.wait_recv()
    for c in pending:
        c.wait_send()


def local(
    hidden_in, norm_gain, norm_bias, w_query, w_key, w_value, w_out,
    prefix_keys, prefix_values, segment, request_group, block_slot, block_live,
):
    rows, width = hidden_in.shape
    lw = w_query.shape[1]
    any_, vm, sm = (pl.BlockSpec(memory_space=s) for s in (pl.ANY, pltpu.VMEM, pltpu.SMEM))
    n = XS * YS
    dma = pltpu.SemaphoreType.DMA
    return pl.pallas_call(
        kernel,
        out_shape=jax.ShapeDtypeStruct((rows, width), bf16),
        in_specs=[any_, vm, vm, any_, any_, any_, any_, any_, any_, vm, sm, sm, sm],
        out_specs=vm,
        scratch_shapes=[
            pltpu.VMEM((rows, width), bf16),
            pltpu.VMEM((width, lw), bf16),
            pltpu.VMEM((width, lw), bf16),
            pltpu.VMEM((width, lw), bf16),
            pltpu.VMEM((lw, width), bf16),
            pltpu.VMEM((rows, width), bf16),
            pltpu.VMEM((XS - 1, UNIT, HD), bf16),
            pltpu.VMEM((ZS, XS, UNIT, HD), bf16),
            pltpu.VMEM((4, TOK, HD), bf16),
            pltpu.VMEM((n, TOK, HD), bf16),
            pltpu.VMEM((8, TOK), f32),
            pltpu.VMEM((n, 8, TOK), f32),
            pltpu.VMEM((n, TOK, HD), bf16),
            pltpu.VMEM((4 * TOK, 2 * HD), bf16),
            pltpu.VMEM((4 * TOK, 2 * HD), bf16),
            pltpu.VMEM((n, TOK, 2 * HD), f32),
            pltpu.VMEM((n, TOK, HD), f32),
            pltpu.VMEM((4, TOK, HD), bf16),
            pltpu.VMEM((4, TOK, HD), bf16),
            pltpu.VMEM((4, TOK, HD), f32),
            pltpu.VMEM((4, TOK, HD), f32),
            pltpu.VMEM((4, TOK, HD), f32),
            pltpu.VMEM((n, TOK, HD), bf16),
            pltpu.VMEM((n, TOK, HD), bf16),
            pltpu.VMEM((n, 8, TOK), f32),
            pltpu.VMEM((n, 8, TOK), f32),
            pltpu.VMEM((4, TOK, HD), bf16),
            pltpu.VMEM((rows, width), f32),
            pltpu.VMEM((CH, rows // 2, width // CH), bf16),
            pltpu.VMEM((CH, rows // 2, width // CH), bf16),
            pltpu.VMEM((CH, rows // 2, width // CH), bf16),
            pltpu.VMEM((CH, rows // 2, width // CH), bf16),
            dma((5,)), dma((XS, 2)), dma((XS,)), dma((XS,)), dma((ZS, XS)), dma((ZS, XS)),
            dma((n,)), dma((n,)), dma((n,)), dma((n,)), dma((n,)), dma((n,)), dma((n,)), dma((n,)),
            dma((3, CH)), dma((3, CH)),
        ],
        compiler_params=pltpu.CompilerParams(collective_id=0, has_side_effects=True),
        name="prefill",
    )(
        hidden_in, norm_gain.reshape(1, width), norm_bias.reshape(1, width),
        w_query, w_key, w_value, w_out, prefix_keys, prefix_values,
        segment, request_group, block_slot, block_live,
    )


def solution(mesh):
    return jax.shard_map(
        local,
        mesh=mesh,
        in_specs=(
            P("blk", None), P(), P(), P(None, "mp"), P(None, "mp"), P(None, "mp"), P("mp", None),
            P("blk", None, "mp"), P("blk", None, "mp"), P("blk", None), P("blk", None), P("blk"), P("blk"),
        ),
        out_specs=P("blk", None),
        check_vma=False,
    )
```

```python
import jax
import jax.numpy as jnp
from jax import lax
from jax.experimental import pallas as pl
from jax.experimental.pallas import tpu as pltpu
from jax.sharding import PartitionSpec as P

MESH = pl.DeviceIdType.MESH
HD = 128
GROUPS = 4
XS, ZS, YS = 4, 8, 2
ROWS = 128
TOK = 128
UNIT = 264
BIG = 1e30
CH = 4
RC = 2

f32 = jnp.float32
bf16 = jnp.bfloat16


def dot_t(a, b):
    return lax.dot_general(a, b, (((1,), (1,)), ((), ())), preferred_element_type=f32)


def kernel(
    hid_hbm, gain_ref, bias_ref, wq_hbm, wk_hbm, wv_hbm, wo_hbm, pk_hbm, pv_hbm,
    seg_ref, rg_ref, slot_ref, live_ref, out_ref,
    hid, wq, wk, wv, wo, nrm, stage, kv, qst, qbuf, gst, gbuf, oh, kc, vc, acc, mx,
    knew, vnew, sacc, smx, stot, rst, rbuf, sst, sbuf, att, part, s1, r1, s2, r2,
    w_sem, st_sem, a_ssem, a_rsem, z_ssem, z_rsem, q_ssem, q_rsem, g_ssem, g_rsem,
    r_ssem, r_rsem, t_ssem, t_rsem, m_ssem, m_rsem,
):
    blk = lax.axis_index("blk")
    mp = lax.axis_index("mp")
    y = blk % YS
    z = (blk // YS) % ZS
    x = blk // (YS * ZS)
    core = mp % 2
    ylo = mp // 2

    def at(px, pz, py):
        return {"blk": (px * ZS + pz) * YS + py}

    def plus(ox, oy):
        return at((x + ox) % XS, z, (y + oy) % YS)

    def minus(ox, oy):
        return at((x + XS - ox) % XS, z, (y + oy) % YS)

    right, left = at(x, (z + 1) % ZS, y), at(x, (z + ZS - 1) % ZS, y)
    mate = {"mp": mp + 1 - 2 * core}
    across = {"mp": mp + 2 - 4 * ylo}
    peers = [(ox, oy) for oy in range(YS) for ox in range(XS) if (ox, oy) != (0, 0)]

    def rdma(src, dst, ssem, rsem, dev):
        return pltpu.make_async_remote_copy(
            src_ref=src, dst_ref=dst, send_sem=ssem, recv_sem=rsem,
            device_id=dev, device_id_type=MESH,
        )

    pending = []

    def send(*args):
        copy = rdma(*args)
        copy.start()
        pending.append(copy)
        return copy

    barrier = pltpu.get_barrier_semaphore()
    friends = [plus(ox, oy) for ox, oy in peers] + [right, left, mate, across]
    for d in friends:
        pl.semaphore_signal(barrier, inc=1, device_id=d, device_id_type=MESH)

    staged = []
    for o in range(XS):
        col = pl.ds(pl.multiple_of(((x + o) % XS) * HD, HD), HD)
        base = kv.at[0, 0] if o == 0 else stage.at[o - 1]
        for i, src in enumerate((pk_hbm, pv_hbm)):
            rows = pl.ds(0, TOK) if i == 0 else pl.ds(TOK + 8, TOK)
            c = pltpu.make_async_copy(src.at[0, :, col], base.at[rows, :], st_sem.at[o, i])
            c.start()
            staged.append(c)
    loads = []
    for i, (src, dst) in enumerate(
        ((hid_hbm, hid), (wq_hbm, wq), (wk_hbm, wk), (wv_hbm, wv), (wo_hbm, wo))
    ):
        c = pltpu.make_async_copy(src, dst, w_sem.at[i])
        c.start()
        loads.append(c)

    tag = jnp.where(live_ref[0] == 1, slot_ref[0] * GROUPS // (XS * ZS * YS), -1)
    lane8 = lax.broadcasted_iota(jnp.int32, (8, HD), 1)
    mask_rows = jnp.where(lane8 == tag, 0.0, -BIG).astype(bf16)
    for o in range(XS):
        if o == 0:
            kv[0, 0, TOK:TOK + 8, :] = mask_rows
        else:
            stage[o - 1, TOK:TOK + 8, :] = mask_rows
    seg = seg_ref[...]
    grp = jnp.zeros((1, TOK), f32)
    for r in range(rg_ref.shape[1]):
        grp = jnp.where(seg == r, rg_ref[0, r].astype(f32), grp)
    grp8 = jnp.broadcast_to(grp, (8, TOK))
    gst[...] = grp8
    gbuf[0] = grp8
    vc[:, HD:] = jnp.ones((4 * TOK, HD), bf16)

    pl.semaphore_wait(barrier, len(friends))

    for c in staged:
        c.wait()
    a2a = {}
    for o in (1, 3, 2):
        a2a[o] = send(stage.at[o - 1], kv.at[0, o], a_ssem.at[o], a_rsem.at[o], plus(o, 0))

    ring = {}

    def push(u, b, to, dev):
        ring[to, b] = send(kv.at[u, b], kv.at[to, b], z_ssem.at[to, b], z_rsem.at[to, b], dev)

    push(0, 0, 1, right)
    push(0, 0, 7, left)
    gcopy = []
    for ox, oy in peers:
        s = oy * XS + ox
        gcopy.append(send(gst, gbuf.at[s], g_ssem.at[s], g_rsem.at[s], plus(ox, oy)))

    loads[0].wait()

    def norm(i, _):
        rows = pl.ds(pl.multiple_of(i * 16, 16), 16)
        v = hid[rows, :].astype(f32)
        c = v - jnp.mean(v, axis=1, keepdims=True)
        var = jnp.mean(c * c, axis=1, keepdims=True)
        nrm[rows, :] = (c * lax.rsqrt(var + 1e-05) * gain_ref[...] + bias_ref[...]).astype(bf16)
        return 0

    lax.fori_loop(0, ROWS // 16, norm, 0)

    loads[1].wait()
    q = jnp.dot(nrm[...], wq[...], preferred_element_type=f32) / jnp.sqrt(f32(HD))
    for h in range(4):
        qst[h] = q[:, h * HD:(h + 1) * HD].astype(bf16)
    qbuf[0] = qst[x]
    qcopy = []
    for ox, oy in peers:
        s = oy * XS + ox
        qcopy.append(
            send(qst.at[(x + ox) % XS], qbuf.at[s], q_ssem.at[s], q_rsem.at[s], plus(ox, oy))
        )

    def forward(d, b):
        ring[d, b].wait_recv()
        if d < 3 or b in (0, 3):
            push(d, b, d + 1, right)
        ring[8 - d, b].wait_recv()
        if d < 3 or b in (1, 2):
            push(8 - d, b, 7 - d, left)

    def land(b):
        ring[4, b].wait_recv()

    forward(1, 0)
    for b in (1, 3, 2):
        a2a[b].wait_recv()
        push(0, b, 1, right)
        push(0, b, 7, left)
    loads[2].wait()
    k = jnp.dot(nrm[...], wk[...], preferred_element_type=f32)
    for h in range(4):
        knew[h] = k[:, h * HD:(h + 1) * HD].astype(bf16)
    forward(2, 0)
    loads[3].wait()
    v = jnp.dot(nrm[...], wv[...], preferred_element_type=f32)
    for h in range(4):
        vnew[h] = v[:, h * HD:(h + 1) * HD].astype(bf16)
    forward(1, 1)
    segb = jnp.broadcast_to(seg.astype(f32), (TOK, TOK))
    segt = segb.T
    row_i = lax.broadcasted_iota(jnp.int32, (TOK, TOK), 0)
    col_i = lax.broadcasted_iota(jnp.int32, (TOK, TOK), 1)
    own = (segb == segt) & (col_i <= row_i)
    for h in range(4):
        s = jnp.where(own, dot_t(qst[h], knew[h]), -BIG)
        top = jnp.max(s, axis=1, keepdims=True)
        w = jnp.where(own, jnp.exp(s - top), 0.0)
        stot[h] = jnp.broadcast_to(jnp.sum(w, axis=1, keepdims=True), (TOK, HD))
        smx[h] = jnp.broadcast_to(top, (TOK, HD))
        sacc[h] = jnp.dot(w.astype(bf16), vnew[h], preferred_element_type=f32)

    forward(1, 3)
    for c in gcopy:
        c.wait_recv()
    for s in range(XS * YS):
        hot = jnp.broadcast_to(gbuf[s][0:1, :], (TOK, TOK)) == row_i.astype(f32)
        oh[s] = jnp.where(hot, 1.0, 0.0).T.astype(bf16)

    acc[...] = jnp.zeros_like(acc)
    mx[...] = jnp.full_like(mx, -3e38)
    for c in qcopy:
        c.wait_recv()

    def attend(blocks, after=None):
        for i, (u, b) in enumerate(blocks):
            rows = slice(i * TOK, (i + 1) * TOK)
            kc[rows, 0:HD] = kv[u, b, 0:TOK, :]
            kc[rows, HD:] = jnp.concatenate([kv[u, b, TOK:TOK + 8, :]] * 16, axis=0)
            vc[rows, 0:HD] = kv[u, b, TOK + 8:UNIT, :]

        def score(r):
            pair = slice(r * RC, (r + 1) * RC)
            n = RC * TOK
            qq = jnp.concatenate([qbuf[pair].reshape(n, HD), oh[pair].reshape(n, HD)], axis=1)
            return dot_t(qq, kc[...])

        def update(r, s):
            pair = slice(r * RC, (r + 1) * RC)
            n = RC * TOK
            old = mx[pair].reshape(n, HD)
            new = jnp.maximum(old, jnp.broadcast_to(jnp.max(s, axis=1, keepdims=True), old.shape))
            w = jnp.exp(s - jnp.concatenate([new] * 4, axis=1)).astype(bf16)
            keep = jnp.exp(old - new)
            res = acc[pair].reshape(n, 2 * HD) * jnp.concatenate([keep, keep], axis=1) + jnp.dot(
                w, vc[...], preferred_element_type=f32
            )
            acc[pair] = res.reshape(RC, TOK, 2 * HD)
            mx[pair] = new.reshape(RC, TOK, HD)

        steps = XS * YS // RC
        ahead = score(steps - 1)
        for r in range(steps - 1, -1, -1):
            s, ahead = ahead, score(r - 1) if r else None
            update(r, s)
            if after is not None:
                after(range((r + 1) * RC - 1, r * RC - 1, -1))

    lane = lax.broadcasted_iota(jnp.int32, (TOK, HD), 1)
    back = []

    def give_back(rows):
        for s in rows:
            res = acc[s]
            stats = jnp.where(lane == 0, mx[s], res[:, HD:]).T[0:8, :]
            if s == 0:
                rbuf[0] = res[:, :HD].astype(bf16)
                sbuf[0] = stats
            else:
                rst[s] = res[:, :HD].astype(bf16)
                sst[s] = stats
                dev = minus(s % XS, s // XS)
                back.append(send(rst.at[s], rbuf.at[s], r_ssem.at[s], r_rsem.at[s], dev))
                back.append(send(sst.at[s], sbuf.at[s], t_ssem.at[s], t_rsem.at[s], dev))

    attend([(0, 0), (0, 1), (0, 3), (0, 2)])
    forward(1, 2)
    forward(3, 0)
    attend([(1, 0), (7, 0), (2, 0), (6, 0)])
    forward(2, 1)
    attend([(1, 1), (7, 1), (1, 3), (7, 3)])
    forward(2, 3)
    forward(2, 2)
    attend([(1, 2), (7, 2), (3, 0), (5, 0)])
    forward(3, 1)
    attend([(2, 1), (6, 1), (2, 3), (6, 3)])
    forward(3, 3)
    attend([(2, 2), (6, 2), (3, 1), (5, 1)])
    forward(3, 2)
    land(0)
    land(1)
    attend([(3, 3), (5, 3), (4, 0), (4, 1)])
    land(3)
    land(2)
    attend([(3, 2), (5, 2), (4, 3), (4, 2)], give_back)
    for c in pending:
        c.wait_send()
    pending.clear()
    for c in back:
        c.wait_recv()
    st = sbuf[...].reshape(8 * XS * YS, TOK)
    st = jnp.concatenate([st, st], axis=0).T
    for ox in range(XS):
        h = (x + ox) % XS
        i, j = 8 * ox, 8 * (XS + ox)
        m1, l1 = st[:, i:i + 1], st[:, i + 1:i + 2]
        m2, l2 = st[:, j:j + 1], st[:, j + 1:j + 2]
        m3, l3 = smx[h], stot[h]
        top = jnp.maximum(jnp.maximum(m1, m2), m3)
        e1, e2, e3 = jnp.exp(m1 - top), jnp.exp(m2 - top), jnp.exp(m3 - top)
        num = rbuf[ox].astype(f32) * e1 + rbuf[XS + ox].astype(f32) * e2 + sacc[h] * e3
        att[h] = (num / (l1 * e1 + l2 * e2 + l3 * e3)).astype(bf16)

    loads[4].wait()
    attended = jnp.concatenate([att[h] for h in range(4)], axis=1)
    half = ROWS // 2
    mine = pl.ds(pl.multiple_of(core * half, half), half)
    other = pl.ds(pl.multiple_of((1 - core) * half, half), half)
    wide = out_ref.shape[1] // CH
    cols = [slice(c * wide, (c + 1) * wide) for c in range(CH)]
    first, second, third = [], [], []
    for c in range(CH):
        part[:, cols[c]] = jnp.dot(attended, wo[:, cols[c]], preferred_element_type=f32)
        s1[c] = part[other, cols[c]].astype(bf16)
        first.append(send(s1.at[c], r1.at[c], m_ssem.at[0, c], m_rsem.at[0, c], mate))
    for c in range(CH):
        first[c].wait_recv()
        s2[c] = (part[mine, cols[c]] + r1[c].astype(f32)).astype(bf16)
        second.append(send(s2.at[c], r2.at[c], m_ssem.at[1, c], m_rsem.at[1, c], across))
    for c in range(CH):
        second[c].wait_recv()
        total = s2[c].astype(f32) + r2[c].astype(f32)
        out_ref[mine, cols[c]] = total.astype(out_ref.dtype)
        spot = out_ref.at[mine, pl.ds(c * wide, wide)]
        third.append(send(spot, spot, m_ssem.at[2, c], m_rsem.at[2, c], mate))
    for c in third:
        c.wait_recv()
    for c in pending:
        c.wait_send()


def local(
    hidden_in, norm_gain, norm_bias, w_query, w_key, w_value, w_out,
    prefix_keys, prefix_values, segment, request_group, block_slot, block_live,
):
    rows, width = hidden_in.shape
    lw = w_query.shape[1]
    any_, vm, sm = (pl.BlockSpec(memory_space=s) for s in (pl.ANY, pltpu.VMEM, pltpu.SMEM))
    n = XS * YS
    dma = pltpu.SemaphoreType.DMA
    branch = pl.pallas_call(
        kernel,
        out_shape=pltpu.VMEM((rows, width), bf16),
        in_specs=[any_, vm, vm, any_, any_, any_, any_, any_, any_, vm, sm, sm, sm],
        out_specs=vm,
        scratch_shapes=[
            pltpu.VMEM((rows, width), bf16),
            pltpu.VMEM((width, lw), bf16),
            pltpu.VMEM((width, lw), bf16),
            pltpu.VMEM((width, lw), bf16),
            pltpu.VMEM((lw, width), bf16),
            pltpu.VMEM((rows, width), bf16),
            pltpu.VMEM((XS - 1, UNIT, HD), bf16),
            pltpu.VMEM((ZS, XS, UNIT, HD), bf16),
            pltpu.VMEM((4, TOK, HD), bf16),
            pltpu.VMEM((n, TOK, HD), bf16),
            pltpu.VMEM((8, TOK), f32),
            pltpu.VMEM((n, 8, TOK), f32),
            pltpu.VMEM((n, TOK, HD), bf16),
            pltpu.VMEM((4 * TOK, 2 * HD), bf16),
            pltpu.VMEM((4 * TOK, 2 * HD), bf16),
            pltpu.VMEM((n, TOK, 2 * HD), f32),
            pltpu.VMEM((n, TOK, HD), f32),
            pltpu.VMEM((4, TOK, HD), bf16),
            pltpu.VMEM((4, TOK, HD), bf16),
            pltpu.VMEM((4, TOK, HD), f32),
            pltpu.VMEM((4, TOK, HD), f32),
            pltpu.VMEM((4, TOK, HD), f32),
            pltpu.VMEM((n, TOK, HD), bf16),
            pltpu.VMEM((n, TOK, HD), bf16),
            pltpu.VMEM((n, 8, TOK), f32),
            pltpu.VMEM((n, 8, TOK), f32),
            pltpu.VMEM((4, TOK, HD), bf16),
            pltpu.VMEM((rows, width), f32),
            pltpu.VMEM((CH, rows // 2, width // CH), bf16),
            pltpu.VMEM((CH, rows // 2, width // CH), bf16),
            pltpu.VMEM((CH, rows // 2, width // CH), bf16),
            pltpu.VMEM((CH, rows // 2, width // CH), bf16),
            dma((5,)), dma((XS, 2)), dma((XS,)), dma((XS,)), dma((ZS, XS)), dma((ZS, XS)),
            dma((n,)), dma((n,)), dma((n,)), dma((n,)), dma((n,)), dma((n,)), dma((n,)), dma((n,)),
            dma((3, CH)), dma((3, CH)),
        ],
        compiler_params=pltpu.CompilerParams(collective_id=0, has_side_effects=True),
        name="prefill",
    )(
        hidden_in, norm_gain.reshape(1, width), norm_bias.reshape(1, width),
        w_query, w_key, w_value, w_out, prefix_keys, prefix_values,
        segment, request_group, block_slot, block_live,
    )
    return (hidden_in.astype(f32) + branch.astype(f32)).astype(bf16)


def solution(mesh):
    return jax.shard_map(
        local,
        mesh=mesh,
        in_specs=(
            P("blk", None), P(), P(), P(None, "mp"), P(None, "mp"), P(None, "mp"), P("mp", None),
            P("blk", None, "mp"), P("blk", None, "mp"), P("blk", None), P("blk", None), P("blk"), P("blk"),
        ),
        out_specs=P("blk", None),
        check_vma=False,
    )
```
